32 devices in a mesh: groups: 2 (over y), seq: 4 (over z), head: 2 (over x), rep: 2 (over core).
Axes of the slice: x: 2, y: 2, z: 4, core: 2. Of those that a mesh axis runs over, the one named last changes fastest.
Arguments:
- document_query: bfloat16 [4096, 8192], P(('groups', 'seq', 'rep'), 'head'), parts along dimension 0, may hold values from -6 to 6
- document_key: bfloat16 [4096, 8192], P(('groups', 'seq', 'rep'), 'head'), parts along dimension 0, may hold values from -0.059814453 to 0.059814453
- document_value: bfloat16 [4096, 8192], P(('groups', 'seq', 'rep'), 'head'), parts along dimension 0, may hold values from -6 to 6
- document_decay: float32 [4096, 64], P(('groups', 'seq', 'rep'), 'head'), parts along dimension 0, may hold values from 0 to 1, as said below
- passage_query: bfloat16 [16, 256, 8192], P(('groups', 'seq', 'rep'), None, 'head'), parts along dimension 0, may hold values from -6 to 6
- passage_key: bfloat16 [16, 256, 8192], P(('groups', 'seq', 'rep'), None, 'head'), parts along dimension 0, may hold values from -0.059814453 to 0.059814453
- passage_value: bfloat16 [16, 256, 8192], P(('groups', 'seq', 'rep'), None, 'head'), parts along dimension 0, may hold values from -6 to 6
- passage_gate: bfloat16 [16, 256, 8192], P(('groups', 'seq', 'rep'), None, 'head'), parts along dimension 0, may hold values from -8 to 8
- passage_decay: float32 [16, 256, 64], P(('groups', 'seq', 'rep'), None, 'head'), parts along dimension 0, may hold values from 0 to 1, as said below
- passage_length: int32 [16], P(('groups', 'seq', 'rep')), parts along dimension 0, may hold values from 64 to 256, as said below
- norm_gain: float32 [8192], P('head'), may hold values from 0.1 to 1.9
Outputs:
- document_output: bfloat16 [4096, 8192], P(('groups', 'seq', 'rep'), 'head'), parts along dimension 0
- passage_output: bfloat16 [16, 256, 8192], P(('groups', 'seq', 'rep'), None, 'head'), parts along dimension 0
The draws below stay inside these ranges and needn't reach their ends.
There are 2 independent parts, one for each index of `groups`. The reference program is written for one: setup_inputs(seed, part) draws one part's arguments, and reference() takes and returns one part's arrays. A program takes and returns all parts, laid end to end along the dimension named above; an argument that names none is the same for every part. Nothing has to cross between parts.
Inputs may be any that keep to these rules, and one draw needn't show every extreme that they name: `document_decay`: positive per-position log-decay rates. `passage_decay`: positive per-position log-decay rates. `passage_length`: a passage's valid tokens are its first ones.
All inputs are finite; a program needn't handle non-finite values.
Results may differ from the reference program's by a relative error of at most 0.0046.
Values sent between devices are 32-bit elements; how exact they have to be, the bound alone decides.
A program may use at most 128 MiB of HBM per device.

```python
import jax
import jax.numpy as jnp
from jax import lax

HEADS = 64
HD = 128
DOC_DEV = 256
PLEN = 256
DOC = 2048
PASSAGES = 8


def decay_formula(key, total_count, block_span, linked_sequence, surge_events):
    key_rows = jax.random.split(key, 7)
    share = 0.5
    slow = jax.random.uniform(key_rows[0], (HEADS,)) < share
    slow_rate = jnp.exp(jax.random.uniform(key_rows[1], (HEADS,), minval=jnp.log(0.05), maxval=jnp.log(0.3))) / linked_sequence
    fast_rate = jnp.exp(jax.random.uniform(key_rows[2], (HEADS,), minval=jnp.log(1.0 / 50.0), maxval=jnp.log(1.0 / 30.0)))
    rate = jnp.where(slow, slow_rate, fast_rate)
    factor = jnp.exp(jax.random.uniform(key_rows[3], (total_count // block_span, 1), minval=jnp.log(0.5), maxval=jnp.log(2.0)))
    factor = jnp.repeat(factor, block_span, axis=0)
    rough = jax.random.uniform(key_rows[4], (total_count, HEADS), minval=0.5, maxval=1.5)
    step_spacing = total_count // surge_events
    surge_position = jnp.arange(surge_events) * step_spacing + jax.random.randint(key_rows[5], (surge_events,), 0, step_spacing)
    intensity = jax.random.uniform(key_rows[6], (surge_events,), minval=0.22, maxval=0.69)
    match_tally = jnp.dot((jnp.arange(total_count)[:, None] == surge_position[None, :]).astype(jnp.float32), intensity)
    return (rate[None, :] * factor * rough + match_tally[:, None]).astype(jnp.float32)


def draw_document_decay(key, part):
    return decay_formula(jax.random.fold_in(key, 11), DOC, DOC_DEV, DOC, 3)


def draw_passage_decay(key, part):
    rates = decay_formula(jax.random.fold_in(key, 12), PASSAGES * PLEN, PLEN, PLEN, PASSAGES)
    return rates.reshape(PASSAGES, PLEN, HEADS)


def draw_passage_length(key, part):
    lengths = jax.random.randint(jax.random.fold_in(key, 13), (PASSAGES,), PLEN // 4, PLEN + 1)
    lengths = lengths.at[0].set(PLEN).at[PASSAGES - 1].set(PLEN // 4)
    return lengths.astype(jnp.int32)


def steps_of(rng, shape, cuts, low, largest):
    def one(dim, shards_of):
        heights = jax.random.uniform(jax.random.fold_in(jax.random.fold_in(rng, 6), dim), (shards_of,), jnp.float32, low / len(cuts), largest / len(cuts))
        return jnp.repeat(jnp.exp(heights), shape[dim] // shards_of).reshape((-1,) + (1,) * (len(shape) - dim - 1))

    factor_of = one(*cuts[0])
    for cut in cuts[1:]:
        factor_of = factor_of * one(*cut)
    return factor_of


def normal_values(stream_key, dims, scale, reach, cuts=(), held_as=jnp.bfloat16):
    entries = jax.random.normal(stream_key, dims, jnp.float32) * scale
    if len(cuts) > 0:
        entries = steps_of(stream_key, dims, cuts, -0.22, 0.18) * entries
    return jnp.clip(entries, min=-reach, max=reach).astype(held_as)


def setup_inputs(seed: int = 0, part: int = 0) -> dict:
    seeds = jax.random.split(jax.random.key(seed), 12)
    own_keys = jax.random.split(jax.random.fold_in(seeds[11], part), 12)
    document_query = normal_values(own_keys[0], (DOC, HEADS * HD), 1.0, 6.0, ((0, 8), (1, 2)))
    document_key = normal_values(own_keys[1], (DOC, HEADS * HD), 0.01, 0.059814453, ((0, 8), (1, 2)))
    document_value = normal_values(own_keys[2], (DOC, HEADS * HD), 1.0, 6.0, ((0, 8), (1, 2)))
    document_decay = draw_document_decay(jax.random.fold_in(jax.random.fold_in(seeds[11], part), 71), part)
    passage_query = normal_values(own_keys[4], (PASSAGES, PLEN, HEADS * HD), 1.0, 6.0, ((0, 8), (2, 2)))
    passage_key = normal_values(own_keys[5], (PASSAGES, PLEN, HEADS * HD), 0.01, 0.059814453, ((0, 8), (2, 2)))
    passage_value = normal_values(own_keys[6], (PASSAGES, PLEN, HEADS * HD), 1.0, 6.0, ((0, 8), (2, 2)))
    passage_gate = normal_values(own_keys[7], (PASSAGES, PLEN, HEADS * HD), 2.0, 8.0, ((0, 8), (2, 2)))
    passage_decay = draw_passage_decay(jax.random.fold_in(jax.random.fold_in(seeds[11], part), 71), part)
    passage_length = draw_passage_length(jax.random.fold_in(jax.random.fold_in(seeds[11], part), 71), part)
    norm_gain = jnp.clip(1.0 + 0.18 * jax.random.normal(seeds[10], (HEADS * HD,), jnp.float32), 0.1, 1.9)
    return dict(document_query=document_query, document_key=document_key, document_value=document_value, document_decay=document_decay, passage_query=passage_query, passage_key=passage_key, passage_value=passage_value, passage_gate=passage_gate, passage_decay=passage_decay, passage_length=passage_length, norm_gain=norm_gain)


epsilon = 1e-05

def block_attend(queries, keys_in, values_in, rates, entering):
    length = queries.shape[0]
    cumulative = jnp.cumsum(rates, axis=0)
    scores = jnp.einsum('thd,shd->hts', queries.astype(jnp.float32), keys_in.astype(jnp.float32))
    ordered = jnp.transpose(cumulative)
    spread = ordered[:, None, :] - ordered[:, :, None]
    causal = (jnp.arange(length)[:, None] >= jnp.arange(length)[None, :])[None]
    weights = jnp.where(causal, scores * jnp.exp(jnp.where(causal, spread, 0.0)), 0.0).astype(jnp.bfloat16)
    intra_part = jnp.einsum('hts,shd->thd', weights.astype(jnp.float32), values_in.astype(jnp.float32))
    inter_part = jnp.einsum('thd,hde->the', queries.astype(jnp.float32), entering.astype(jnp.float32), precision=lax.Precision.HIGHEST)
    inter_part = inter_part * jnp.exp(-cumulative)[:, :, None]
    closing = cumulative[-1]
    scaled_key = (keys_in.astype(jnp.float32) * jnp.exp(cumulative - closing[None, :])[:, :, None]).astype(jnp.bfloat16)
    state = jnp.einsum('shd,she->hde', scaled_key.astype(jnp.float32), values_in.astype(jnp.float32))
    return (intra_part + inter_part, state, jnp.exp(-closing))

def reference(document_query, document_key, document_value, document_decay, passage_query, passage_key, passage_value, passage_gate, passage_decay, passage_length, norm_gain):
    blocks = DOC // DOC_DEV
    block_shape = (blocks, DOC_DEV, HEADS, HD)

    def advance(entering, inputs):
        queries, keys_in, values_in, rates = inputs
        attended, state, decay = block_attend(queries, keys_in, values_in, rates, entering)
        return (decay[:, None, None] * entering + state, attended.astype(jnp.bfloat16))
    memory, outputs = lax.scan(advance, jnp.zeros((HEADS, HD, HD), jnp.float32), (document_query.reshape(block_shape), document_key.reshape(block_shape), document_value.reshape(block_shape), document_decay.reshape(blocks, DOC_DEV, HEADS)))
    document_output = outputs.reshape(DOC, HEADS * HD)

    def readout(inputs):
        queries, keys_in, values_in, gate, rates, valid = inputs
        attended, unused_state, unused_decay = block_attend(queries.reshape(PLEN, HEADS, HD), keys_in.reshape(PLEN, HEADS, HD), values_in.reshape(PLEN, HEADS, HD), rates, memory)
        flat = attended.reshape(PLEN, HEADS * HD)
        mean_square = lax.optimization_barrier(jnp.mean(flat * flat, axis=1, keepdims=True))
        normed = flat * lax.rsqrt(mean_square + epsilon) * norm_gain[None, :] * jax.nn.sigmoid(gate.astype(jnp.float32))
        inside = (jnp.arange(PLEN) < valid)[:, None]
        return jnp.where(inside, normed, 0.0).astype(jnp.bfloat16)
    passage_output = lax.map(readout, (passage_query, passage_key, passage_value, passage_gate, passage_decay, passage_length))
    return (document_output, passage_output)
```

```python
import functools

import jax
import jax.numpy as jnp
from jax import lax
from jax.experimental import pallas as pl
from jax.experimental.pallas import tpu as pltpu
from jax.sharding import PartitionSpec as P

epsilon = 1e-05
LAG = 2
MESH = pl.DeviceIdType.MESH


def column(row, lanes):
    length = row.shape[1]
    parts = [
        jnp.transpose(jnp.broadcast_to(row[:, a : a + lanes], (lanes, lanes)))
        for a in range(0, length, lanes)
    ]
    return jnp.concatenate(parts, axis=0)


def exact_dot(queries, state):
    high = state.astype(jnp.bfloat16)
    low = (state - high.astype(jnp.float32)).astype(jnp.bfloat16)
    return jnp.dot(
        jnp.concatenate([queries, queries], axis=1),
        jnp.concatenate([high, low], axis=0),
        preferred_element_type=jnp.float32,
    )


def kernel(
    n,
    hn,
    heads,
    hd,
    q_hbm,
    k_hbm,
    v_hbm,
    decay_ref,
    pq_hbm,
    pk_hbm,
    pv_hbm,
    pg_hbm,
    pdecay_ref,
    plen_ref,
    gain_ref,
    out_hbm,
    pout_hbm,
    q,
    k,
    v,
    pq,
    pk,
    pv,
    pg,
    dob,
    pob,
    dintra,
    pintra,
    cum_t,
    pcum_t,
    closings,
    d0_t,
    d1_t,
    dsuf_t,
    s_out,
    s_own,
    s_in,
    s_first,
    s_chip,
    f_in,
    f_out,
    b_in,
    b_out,
    e_own,
    e_out,
    e_in,
    m_out,
    m_in,
    acc,
    sq,
    scale,
    load_sem,
    store_sem,
    close_send,
    close_recv,
    pair_send,
    pair_recv,
    line_send,
    line_recv,
    sq_send,
    sq_recv,
):
    c, r, hx = lax.axis_index("seq"), lax.axis_index("rep"), lax.axis_index("head")
    rows = q.shape[0]
    prow = pq.shape[0]
    count = heads // 2
    blocks = 2 * n
    b = c * 2 + r
    f32 = jnp.float32
    high = lax.Precision.HIGHEST

    loads = [
        pltpu.make_async_copy(src, dst, load_sem.at[i])
        for i, (src, dst) in enumerate(
            [
                (k_hbm, k),
                (v_hbm, v),
                (q_hbm, q),
                (pk_hbm, pk),
                (pq_hbm, pq),
                (pv_hbm, pv),
                (pg_hbm, pg),
            ]
        )
    ]
    for load in loads:
        load.start()

    barrier = pltpu.get_barrier_semaphore()
    line = []
    for step in range(1, blocks):
        to = lax.rem(b + step, blocks)
        line.append({"seq": to // 2, "rep": lax.rem(to, 2)})
    across = [{"head": lax.rem(hx + step, hn)} for step in range(1, hn)]
    for peer in line + across:
        pl.semaphore_signal(barrier, inc=1, device_id=peer, device_id_type=MESH)

    def upper(length):
        return (
            lax.broadcasted_iota(jnp.int32, (length, length), 0)
            <= lax.broadcasted_iota(jnp.int32, (length, length), 1)
        ).astype(f32)

    contract_rows = (((0,), (0,)), ((), ()))
    contract_lanes = (((1,), (1,)), ((), ()))
    rates = decay_ref[...]
    sums = jnp.dot(jnp.ones((8, rows), f32), rates, precision=high, preferred_element_type=f32)
    closings[b] = jnp.zeros((1, hd), f32)
    closings[b, :, :heads] = sums[0:1]
    cum_t[...] = lax.dot_general(
        rates, upper(rows), contract_rows, precision=high, preferred_element_type=f32
    )
    pcum_t[...] = lax.dot_general(
        pdecay_ref[...], upper(prow), contract_rows, precision=high, preferred_element_type=f32
    )
    acc[...] = jnp.zeros_like(acc)

    @pl.when(c == 0)
    def _():
        f_in[...] = jnp.zeros_like(f_in)

    @pl.when(c == n - 1)
    def _():
        b_in[...] = jnp.zeros_like(b_in)

    pl.semaphore_wait(barrier, len(line) + len(across))

    close_copies = [
        pltpu.make_async_remote_copy(
            src_ref=closings.at[b],
            dst_ref=closings.at[b],
            send_sem=close_send.at[i],
            recv_sem=close_recv.at[i],
            device_id=peer,
            device_id_type=MESH,
        )
        for i, peer in enumerate(line)
    ]
    for copy in close_copies:
        copy.start()

    def pair_copy(kind, src, dst, j):
        return pltpu.make_async_remote_copy(
            src_ref=src.at[j],
            dst_ref=dst.at[j],
            send_sem=pair_send.at[kind, j],
            recv_sem=pair_recv.at[kind, j],
            device_id={"rep": 1 - r},
            device_id_type=MESH,
        )

    def line_copy(kind, src, dst, j, to):
        return pltpu.make_async_remote_copy(
            src_ref=src.at[j],
            dst_ref=dst.at[j],
            send_sem=line_send.at[kind, j],
            recv_sem=line_recv.at[kind, j],
            device_id={"seq": to},
            device_id_type=MESH,
        )

    def state_copy(j):
        return pair_copy(0, s_out, s_in, j)

    def entering_copy(j):
        return pair_copy(1, e_out, e_in, j)

    def memory_copy(j):
        return pair_copy(2, m_out, m_in, j)

    right, left = jnp.minimum(c + 1, n - 1), jnp.maximum(c - 1, 0)

    def forward_copy(j):
        return line_copy(0, f_out, f_in, j, right)

    def backward_copy(j):
        return line_copy(1, b_out, b_in, j, left)

    def lanes_of(h):
        return pl.ds(pl.multiple_of(h * hd, hd), hd)

    def own_head(j):
        return r * count + j

    def other_head(j):
        return (1 - r) * count + j

    def state_of(h):
        col = column(cum_t[pl.ds(h, 1), :], hd)
        scaled = (k[:, lanes_of(h)].astype(f32) * jnp.exp(col - col[rows - 1 : rows, :])).astype(
            jnp.bfloat16
        )
        return lax.dot_general(scaled, v[:, lanes_of(h)], contract_rows, preferred_element_type=f32)

    def intra(qs, ks, vs, cums, into, h):
        length = qs.shape[0]
        qh, kh, vh = qs[:, lanes_of(h)], ks[:, lanes_of(h)], vs[:, lanes_of(h)]
        row = cums[pl.ds(h, 1), :]
        col = column(row, hd)
        pieces = []
        for t in range(0, length, hd):
            ends = t + hd
            scores = lax.dot_general(
                qh[t:ends], kh[:ends], contract_lanes, preferred_element_type=f32
            )
            parts = []
            for s in range(0, ends, hd):
                part = scores[:, s : s + hd] * jnp.exp(row[:, s : s + hd] - col[t:ends])
                if s == t:
                    causal = lax.broadcasted_iota(jnp.int32, (hd, hd), 0) >= (
                        lax.broadcasted_iota(jnp.int32, (hd, hd), 1)
                    )
                    part = jnp.where(causal, part, 0.0)
                parts.append(part.astype(jnp.bfloat16))
            weights = jnp.concatenate(parts, axis=1)
            pieces.append(jnp.dot(weights, vh[:ends], preferred_element_type=f32))
        into[h] = jnp.concatenate(pieces, axis=0)

    def finish(h, entering, memory):
        grow = column(jnp.exp(-cum_t[pl.ds(h, 1), :]), hd)
        at = lanes_of(h)
        dob[:, at] = (dintra[h] + grow * exact_dot(q[:, at], entering)).astype(dob.dtype)
        pltpu.make_async_copy(dob.at[:, at], out_hbm.at[:, at], store_sem.at[0]).start()
        pgrow = column(jnp.exp(-pcum_t[pl.ds(h, 1), :]), hd)
        attended = pintra[h] + pgrow * exact_dot(pq[:, at], memory)
        acc[...] += attended * attended
        pintra[h] = attended * (gain_ref[:, at] * jax.nn.sigmoid(pg[:, at].astype(f32)))

    last = jnp.maximum(c, n - 1 - c) * LAG

    @pl.loop(0, count + (n - 1) * LAG + 2)
    def _(it):
        @pl.when(it == 0)
        def _():
            loads[0].wait()
            loads[1].wait()

        @pl.when(it == 1)
        def _():
            for copy in close_copies:
                copy.wait_recv()
            later = jnp.zeros((1, hd), f32)
            for at in range(2, blocks):
                later = later + jnp.where(at >= 2 * (c + 1), closings[at], 0.0)

            def table(values):
                return jnp.transpose(jnp.broadcast_to(jnp.exp(-values), (hd, hd)))

            d0_t[...] = table(closings[2 * c])
            d1_t[...] = table(closings[2 * c + 1])
            dsuf_t[...] = table(later)

        j0 = it - 1

        @pl.when((j0 >= 0) & (j0 < count))
        def _():
            state_copy(j0).wait_recv()
            one = jnp.where(r == 0, s_own[j0], s_in[j0])
            two = jnp.where(r == 0, s_in[j0], s_own[j0])
            s_first[j0] = one
            s_chip[j0] = d1_t[pl.ds(own_head(j0), 1), :] * one + two

        jf = it - 1 - c * LAG

        @pl.when((jf >= 0) & (jf < count))
        def _():
            h = own_head(jf)

            @pl.when(c > 0)
            def _():
                forward_copy(jf).wait_recv()

            before = f_in[jf]
            d0, d1 = d0_t[pl.ds(h, 1), :], d1_t[pl.ds(h, 1), :]
            f_out[jf] = (d0 * d1) * before + s_chip[jf]

            @pl.when(c < n - 1)
            def _():
                forward_copy(jf).start()

            second = d0 * before + s_first[jf]
            e_own[jf] = jnp.where(r == 0, before, second)
            e_out[jf] = jnp.where(r == 0, second, before)
            entering_copy(jf).start()

        jb = it - 1 - (n - 1 - c) * LAG

        @pl.when((jb >= 0) & (jb < count))
        def _():
            @pl.when(c < n - 1)
            def _():
                backward_copy(jb).wait_recv()

            @pl.when(c > 0)
            def _():
                b_out[jb] = dsuf_t[pl.ds(own_head(jb), 1), :] * s_chip[jb] + b_in[jb]
                backward_copy(jb).start()

        @pl.when(it < count)
        def _():
            s_out[it] = state_of(other_head(it))
            state_copy(it).start()
            s_own[it] = state_of(own_head(it))

        jm = it - 1 - last

        @pl.when((jm >= 0) & (jm < count))
        def _():
            h = own_head(jm)
            memory = dsuf_t[pl.ds(h, 1), :] * f_out[jm] + b_in[jm]
            m_out[jm] = memory
            memory_copy(jm).start()
            finish(h, e_own[jm], memory)

        @pl.when(it == 0)
        def _():
            for load in loads[2:]:
                load.wait()

        @pl.when(it < count)
        def _():
            for h in (own_head(it), other_head(it)):
                intra(q, k, v, cum_t, dintra, h)
                intra(pq, pk, pv, pcum_t, pintra, h)

        jr = it - 2 - last

        @pl.when((jr >= 0) & (jr < count))
        def _():
            entering_copy(jr).wait_recv()
            memory_copy(jr).wait_recv()
            finish(other_head(jr), e_in[jr], m_in[jr])

    squares = lax.dot_general(
        jnp.ones((8, hd), f32), acc[...], contract_lanes, precision=high, preferred_element_type=f32
    )
    sq[hx] = squares
    sq_copies = [
        pltpu.make_async_remote_copy(
            src_ref=sq.at[hx],
            dst_ref=sq.at[hx],
            send_sem=sq_send.at[i],
            recv_sem=sq_recv.at[i],
            device_id=peer,
            device_id_type=MESH,
        )
        for i, peer in enumerate(across)
    ]
    for copy in sq_copies:
        copy.start()
    for copy in sq_copies:
        copy.wait_recv()
    total = sq[0]
    for at in range(1, hn):
        total = total + sq[at]
    factor = lax.rsqrt(total / (hn * heads * hd) + epsilon)
    inside = lax.broadcasted_iota(jnp.int32, factor.shape, 1) < plen_ref[0]
    scale[...] = column(jnp.where(inside, factor, 0.0)[0:1], hd)

    @pl.loop(0, heads)
    def _(h):
        at = lanes_of(h)
        pob[:, at] = (pintra[h] * scale[...]).astype(pob.dtype)
        pltpu.make_async_copy(pob.at[:, at], pout_hbm.at[:, at], store_sem.at[1]).start()

    for copy in close_copies + sq_copies:
        copy.wait_send()

    @pl.loop(0, count)
    def _(j):
        state_copy(j).wait_send()
        entering_copy(j).wait_send()
        memory_copy(j).wait_send()

        @pl.when(c < n - 1)
        def _():
            forward_copy(j).wait_send()

        @pl.when(c > 0)
        def _():
            backward_copy(j).wait_send()

    pltpu.make_async_copy(dob, out_hbm, store_sem.at[0]).wait()
    pltpu.make_async_copy(pob, pout_hbm, store_sem.at[1]).wait()


def local(sizes, dq, dk, dv, dd, pq, pk, pv, pg, pd, plen, gain):
    n, hn, reps = sizes
    heads = dd.shape[1]
    rows, width = dq.shape
    hd = width // heads
    passages, prow = pq.shape[:2]
    assert passages == 1 and reps == 2 and heads % 2 == 0 and heads <= hd
    count = heads // 2
    f32, bf16 = jnp.float32, jnp.bfloat16
    pq, pk, pv, pg = (x.reshape(prow, width) for x in (pq, pk, pv, pg))
    anywhere = pl.BlockSpec(memory_space=pl.ANY)
    vmem = pl.BlockSpec(memory_space=pltpu.VMEM)
    smem = pl.BlockSpec(memory_space=pltpu.SMEM)
    blocks = n * reps
    chunks = pltpu.VMEM((count, hd, hd), f32)
    dma = pltpu.SemaphoreType.DMA
    out, pout = pl.pallas_call(
        functools.partial(kernel, n, hn, heads, hd),
        out_shape=(
            jax.ShapeDtypeStruct((rows, width), bf16),
            jax.ShapeDtypeStruct((prow, width), bf16),
        ),
        in_specs=[anywhere] * 3 + [vmem] + [anywhere] * 4 + [vmem, smem, vmem],
        out_specs=(anywhere, anywhere),
        scratch_shapes=[pltpu.VMEM((rows, width), bf16)] * 3
        + [pltpu.VMEM((prow, width), bf16)] * 4
        + [pltpu.VMEM((rows, width), bf16), pltpu.VMEM((prow, width), bf16)]
        + [pltpu.VMEM((heads, rows, hd), f32), pltpu.VMEM((heads, prow, hd), f32)]
        + [pltpu.VMEM((heads, rows), f32), pltpu.VMEM((heads, prow), f32)]
        + [pltpu.VMEM((blocks, 1, hd), f32)]
        + [pltpu.VMEM((hd, hd), f32)] * 3
        + [chunks] * 14
        + [pltpu.VMEM((prow, hd), f32), pltpu.VMEM((hn, 8, prow), f32), pltpu.VMEM((prow, hd), f32)]
        + [
            dma((7,)),
            dma((2,)),
            dma((blocks - 1,)),
            dma((blocks - 1,)),
            dma((3, count)),
            dma((3, count)),
            dma((2, count)),
            dma((2, count)),
            dma((max(hn - 1, 1),)),
            dma((max(hn - 1, 1),)),
        ],
        compiler_params=pltpu.CompilerParams(
            collective_id=0, has_side_effects=True, vmem_limit_bytes=60 << 20
        ),
    )(dq, dk, dv, dd, pq, pk, pv, pg, pd.reshape(prow, heads), plen, gain.reshape(1, width))
    return out, pout.reshape(passages, prow, width)


def solution(mesh):
    rows = ("groups", "seq", "rep")
    flat, deep = P(rows, "head"), P(rows, None, "head")
    sizes = tuple(mesh.shape[axis] for axis in ("seq", "head", "rep"))
    return jax.shard_map(
        functools.partial(local, sizes),
        mesh=mesh,
        in_specs=(flat,) * 4 + (deep,) * 5 + (P(rows), P("head")),
        out_specs=(flat, deep),
        check_vma=False,
    )
```

```python
import functools

import jax
import jax.numpy as jnp
from jax import lax
from jax.experimental import pallas as pl
from jax.experimental.pallas import tpu as pltpu
from jax.sharding import PartitionSpec as P

epsilon = 1e-05
LAG = 3
AHEAD = 4
MESH = pl.DeviceIdType.MESH


def column(row, lanes):
    length = row.shape[1]
    parts = [
        jnp.transpose(jnp.broadcast_to(row[:, a : a + lanes], (lanes, lanes)))
        for a in range(0, length, lanes)
    ]
    return jnp.concatenate(parts, axis=0)


def exact_dot(queries, state):
    high = state.astype(jnp.bfloat16)
    low = (state - high.astype(jnp.float32)).astype(jnp.bfloat16)
    return jnp.dot(
        jnp.concatenate([queries, queries], axis=1),
        jnp.concatenate([high, low], axis=0),
        preferred_element_type=jnp.float32,
    )


def kernel(
    n,
    hn,
    heads,
    hd,
    q_hbm,
    k_hbm,
    v_hbm,
    decay_ref,
    pq_hbm,
    pk_hbm,
    pv_hbm,
    pg_hbm,
    pdecay_ref,
    plen_ref,
    gain_ref,
    dob,
    pob,
    q,
    k,
    v,
    pq,
    pk,
    pv,
    pg,
    dintra,
    pintra,
    cum_t,
    pcum_t,
    closings,
    d0_t,
    d1_t,
    dsuf_t,
    s_out,
    s_own,
    s_in,
    s_first,
    s_chip,
    f_in,
    f_out,
    b_in,
    b_out,
    e_own,
    e_out,
    e_in,
    m_out,
    m_in,
    acc,
    sq,
    scale,
    load_sem,
    close_send,
    close_recv,
    pair_send,
    pair_recv,
    line_send,
    line_recv,
    sq_send,
    sq_recv,
):
    c, r, hx = lax.axis_index("seq"), lax.axis_index("rep"), lax.axis_index("head")
    rows = q.shape[0]
    prow = pq.shape[0]
    count = heads // 2
    blocks = 2 * n
    b = c * 2 + r
    f32 = jnp.float32
    high = lax.Precision.HIGHEST

    loads = [
        pltpu.make_async_copy(src, dst, load_sem.at[i])
        for i, (src, dst) in enumerate(
            [
                (k_hbm, k),
                (v_hbm, v),
                (q_hbm, q),
                (pk_hbm, pk),
                (pq_hbm, pq),
                (pv_hbm, pv),
                (pg_hbm, pg),
            ]
        )
    ]
    for load in loads:
        load.start()

    barrier = pltpu.get_barrier_semaphore()
    line = []
    for step in range(1, blocks):
        to = lax.rem(b + step, blocks)
        line.append({"seq": to // 2, "rep": lax.rem(to, 2)})
    across = [{"head": lax.rem(hx + step, hn)} for step in range(1, hn)]
    for peer in line + across:
        pl.semaphore_signal(barrier, inc=1, device_id=peer, device_id_type=MESH)

    def upper(length):
        return (
            lax.broadcasted_iota(jnp.int32, (length, length), 0)
            <= lax.broadcasted_iota(jnp.int32, (length, length), 1)
        ).astype(f32)

    contract_rows = (((0,), (0,)), ((), ()))
    contract_lanes = (((1,), (1,)), ((), ()))
    rates = decay_ref[...]
    sums = lax.dot_general(
        jnp.ones((8, rows), f32), rates, contract_lanes, precision=high, preferred_element_type=f32
    )
    closings[b] = jnp.zeros((1, hd), f32)
    closings[b, :, :heads] = sums[0:1]
    cum_t[...] = jnp.dot(rates, upper(rows), precision=high, preferred_element_type=f32)
    pcum_t[...] = jnp.dot(pdecay_ref[...], upper(prow), precision=high, preferred_element_type=f32)
    acc[...] = jnp.zeros_like(acc)

    @pl.when(c == 0)
    def _():
        f_in[...] = jnp.zeros_like(f_in)

    @pl.when(c == n - 1)
    def _():
        b_in[...] = jnp.zeros_like(b_in)

    pl.semaphore_wait(barrier, len(line) + len(across))

    close_copies = [
        pltpu.make_async_remote_copy(
            src_ref=closings.at[b],
            dst_ref=closings.at[b],
            send_sem=close_send.at[i],
            recv_sem=close_recv.at[i],
            device_id=peer,
            device_id_type=MESH,
        )
        for i, peer in enumerate(line)
    ]
    for copy in close_copies:
        copy.start()

    def pair_copy(kind, src, dst, j):
        return pltpu.make_async_remote_copy(
            src_ref=src.at[j],
            dst_ref=dst.at[j],
            send_sem=pair_send.at[kind, j],
            recv_sem=pair_recv.at[kind, j],
            device_id={"rep": 1 - r},
            device_id_type=MESH,
        )

    def line_copy(kind, src, dst, j, to):
        return pltpu.make_async_remote_copy(
            src_ref=src.at[j],
            dst_ref=dst.at[j],
            send_sem=line_send.at[kind, j],
            recv_sem=line_recv.at[kind, j],
            device_id={"seq": to},
            device_id_type=MESH,
        )

    def state_copy(j):
        return pair_copy(0, s_out, s_in, j)

    def entering_copy(j):
        return pair_copy(1, e_out, e_in, j)

    def memory_copy(j):
        return pair_copy(2, m_out, m_in, j)

    right, left = jnp.minimum(c + 1, n - 1), jnp.maximum(c - 1, 0)

    def forward_copy(j):
        return line_copy(0, f_out, f_in, j, right)

    def backward_copy(j):
        return line_copy(1, b_out, b_in, j, left)

    def lanes_of(h):
        return pl.ds(pl.multiple_of(h * hd, hd), hd)

    def own_head(j):
        return r * count + j

    def other_head(j):
        return (1 - r) * count + j

    def state_of(h):
        col = column(cum_t[pl.ds(h, 1), :], hd)
        scaled = (k[:, lanes_of(h)].astype(f32) * jnp.exp(col - col[rows - 1 : rows, :])).astype(
            jnp.bfloat16
        )
        return lax.dot_general(scaled, v[:, lanes_of(h)], contract_rows, preferred_element_type=f32)

    def intra(qs, ks, vs, cums, into, h):
        length = qs.shape[0]
        qh, kh, vh = qs[:, lanes_of(h)], ks[:, lanes_of(h)], vs[:, lanes_of(h)]
        row = cums[pl.ds(h, 1), :]
        col = column(row, hd)
        pieces = []
        for t in range(0, length, hd):
            ends = t + hd
            scores = lax.dot_general(
                qh[t:ends], kh[:ends], contract_lanes, preferred_element_type=f32
            )
            parts = []
            for s in range(0, ends, hd):
                part = scores[:, s : s + hd] * jnp.exp(row[:, s : s + hd] - col[t:ends])
                if s == t:
                    causal = lax.broadcasted_iota(jnp.int32, (hd, hd), 0) >= (
                        lax.broadcasted_iota(jnp.int32, (hd, hd), 1)
                    )
                    part = jnp.where(causal, part, 0.0)
                parts.append(part.astype(jnp.bfloat16))
            weights = jnp.concatenate(parts, axis=1)
            pieces.append(jnp.dot(weights, vh[:ends], preferred_element_type=f32))
        into[h] = jnp.concatenate(pieces, axis=0)

    def finish(h, entering, memory):
        grow = column(jnp.exp(-cum_t[pl.ds(h, 1), :]), hd)
        at = lanes_of(h)
        dob[:, at] = (dintra[h] + grow * exact_dot(q[:, at], entering)).astype(dob.dtype)
        pgrow = column(jnp.exp(-pcum_t[pl.ds(h, 1), :]), hd)
        attended = pintra[h] + pgrow * exact_dot(pq[:, at], memory)
        acc[...] += attended * attended
        pintra[h] = attended * (gain_ref[:, at] * jax.nn.sigmoid(pg[:, at].astype(f32)))

    def combine(j):
        state_copy(j).wait_recv()
        one = jnp.where(r == 0, s_own[j], s_in[j])
        two = jnp.where(r == 0, s_in[j], s_own[j])
        s_first[j] = one
        s_chip[j] = d1_t[pl.ds(own_head(j), 1), :] * one + two

    def forward(j):
        h = own_head(j)

        @pl.when(c > 0)
        def _():
            forward_copy(j).wait_recv()

        before = f_in[j]
        d0, d1 = d0_t[pl.ds(h, 1), :], d1_t[pl.ds(h, 1), :]
        f_out[j] = (d0 * d1) * before + s_chip[j]

        @pl.when(c < n - 1)
        def _():
            forward_copy(j).start()

        second = d0 * before + s_first[j]
        e_own[j] = jnp.where(r == 0, before, second)
        e_out[j] = jnp.where(r == 0, second, before)
        entering_copy(j).start()

    def backward(j):
        @pl.when(c < n - 1)
        def _():
            backward_copy(j).wait_recv()

        @pl.when(c > 0)
        def _():
            b_out[j] = dsuf_t[pl.ds(own_head(j), 1), :] * s_chip[j] + b_in[j]
            backward_copy(j).start()

    @pl.loop(0, count + AHEAD)
    def _(it):
        @pl.when(it == 0)
        def _():
            loads[0].wait()
            loads[1].wait()

        @pl.when(it < count)
        def _():
            s_out[it] = state_of(other_head(it))
            state_copy(it).start()
            s_own[it] = state_of(own_head(it))

        @pl.when(it == AHEAD)
        def _():
            for copy in close_copies:
                copy.wait_recv()
            later = jnp.zeros((1, hd), f32)
            for at in range(2, blocks):
                later = later + jnp.where(at >= 2 * (c + 1), closings[at], 0.0)

            def table(values):
                return jnp.transpose(jnp.broadcast_to(jnp.exp(-values), (hd, hd)))

            d0_t[...] = table(closings[2 * c])
            d1_t[...] = table(closings[2 * c + 1])
            dsuf_t[...] = table(later)

        @pl.when(it >= AHEAD)
        def _():
            j = it - AHEAD
            combine(j)

            @pl.when(c == 0)
            def _():
                forward(j)

            @pl.when(c == n - 1)
            def _():
                backward(j)

    for load in loads[2:]:
        load.wait()

    last = jnp.maximum(jnp.maximum(c - 1, n - 2 - c), 0) * LAG

    @pl.loop(0, count + max(n - 2, 0) * LAG + 1)
    def _(it):
        jf = it - (c - 1) * LAG

        @pl.when((c > 0) & (jf >= 0) & (jf < count))
        def _():
            forward(jf)

        jb = it - (n - 2 - c) * LAG

        @pl.when((c < n - 1) & (jb >= 0) & (jb < count))
        def _():
            backward(jb)

        @pl.when(it < count)
        def _():
            for h in (own_head(it), other_head(it)):
                intra(q, k, v, cum_t, dintra, h)
                intra(pq, pk, pv, pcum_t, pintra, h)

        jm = it - last

        @pl.when((jm >= 0) & (jm < count))
        def _():
            h = own_head(jm)
            memory = dsuf_t[pl.ds(h, 1), :] * f_out[jm] + b_in[jm]
            m_out[jm] = memory
            memory_copy(jm).start()
            finish(h, e_own[jm], memory)

        jr = it - 1 - last

        @pl.when((jr >= 0) & (jr < count))
        def _():
            entering_copy(jr).wait_recv()
            memory_copy(jr).wait_recv()
            finish(other_head(jr), e_in[jr], m_in[jr])

    squares = lax.dot_general(
        jnp.ones((8, hd), f32), acc[...], contract_lanes, precision=high, preferred_element_type=f32
    )
    sq[hx] = squares
    sq_copies = [
        pltpu.make_async_remote_copy(
            src_ref=sq.at[hx],
            dst_ref=sq.at[hx],
            send_sem=sq_send.at[i],
            recv_sem=sq_recv.at[i],
            device_id=peer,
            device_id_type=MESH,
        )
        for i, peer in enumerate(across)
    ]
    for copy in sq_copies:
        copy.start()
    for copy in sq_copies:
        copy.wait_recv()
    total = sq[0]
    for at in range(1, hn):
        total = total + sq[at]
    factor = lax.rsqrt(total / (hn * heads * hd) + epsilon)
    inside = lax.broadcasted_iota(jnp.int32, factor.shape, 1) < plen_ref[0]
    scale[...] = column(jnp.where(inside, factor, 0.0)[0:1], hd)

    @pl.loop(0, heads)
    def _(h):
        at = lanes_of(h)
        pob[:, at] = (pintra[h] * scale[...]).astype(pob.dtype)

    for copy in close_copies + sq_copies:
        copy.wait_send()

    @pl.loop(0, count)
    def _(j):
        state_copy(j).wait_send()
        entering_copy(j).wait_send()
        memory_copy(j).wait_send()

        @pl.when(c < n - 1)
        def _():
            forward_copy(j).wait_send()

        @pl.when(c > 0)
        def _():
            backward_copy(j).wait_send()


def local(sizes, dq, dk, dv, dd, pq, pk, pv, pg, pd, plen, gain):
    n, hn, reps = sizes
    heads = dd.shape[1]
    rows, width = dq.shape
    hd = width // heads
    passages, prow = pq.shape[:2]
    assert passages == 1 and reps == 2 and heads % 2 == 0 and heads <= hd
    count = heads // 2
    f32, bf16 = jnp.float32, jnp.bfloat16
    pq, pk, pv, pg = (x.reshape(prow, width) for x in (pq, pk, pv, pg))
    anywhere = pl.BlockSpec(memory_space=pl.ANY)
    vmem = pl.BlockSpec(memory_space=pltpu.VMEM)
    smem = pl.BlockSpec(memory_space=pltpu.SMEM)
    blocks = n * reps
    chunks = pltpu.VMEM((count, hd, hd), f32)
    dma = pltpu.SemaphoreType.DMA
    out, pout = pl.pallas_call(
        functools.partial(kernel, n, hn, heads, hd),
        out_shape=(
            pltpu.VMEM((rows, width), bf16),
            pltpu.VMEM((prow, width), bf16),
        ),
        in_specs=[anywhere] * 3 + [vmem] + [anywhere] * 4 + [vmem, smem, vmem],
        out_specs=(vmem, vmem),
        scratch_shapes=[pltpu.VMEM((rows, width), bf16)] * 3
        + [pltpu.VMEM((prow, width), bf16)] * 4
        + [pltpu.VMEM((heads, rows, hd), f32), pltpu.VMEM((heads, prow, hd), f32)]
        + [pltpu.VMEM((heads, rows), f32), pltpu.VMEM((heads, prow), f32)]
        + [pltpu.VMEM((blocks, 1, hd), f32)]
        + [pltpu.VMEM((hd, hd), f32)] * 3
        + [chunks] * 14
        + [pltpu.VMEM((prow, hd), f32), pltpu.VMEM((hn, 8, prow), f32), pltpu.VMEM((prow, hd), f32)]
        + [
            dma((7,)),
            dma((blocks - 1,)),
            dma((blocks - 1,)),
            dma((3, count)),
            dma((3, count)),
            dma((2, count)),
            dma((2, count)),
            dma((max(hn - 1, 1),)),
            dma((max(hn - 1, 1),)),
        ],
        compiler_params=pltpu.CompilerParams(
            collective_id=0, has_side_effects=True, vmem_limit_bytes=50 << 20
        ),
    )(dq, dk, dv, dd.T, pq, pk, pv, pg, pd.reshape(prow, heads).T, plen, gain.reshape(1, width))
    return out, pout.reshape(passages, prow, width)


def solution(mesh):
    rows = ("groups", "seq", "rep")
    flat, deep = P(rows, "head"), P(rows, None, "head")
    sizes = tuple(mesh.shape[axis] for axis in ("seq", "head", "rep"))
    return jax.shard_map(
        functools.partial(local, sizes),
        mesh=mesh,
        in_specs=(flat,) * 4 + (deep,) * 5 + (P(rows), P("head")),
        out_specs=(flat, deep),
        check_vma=False,
    )
```

```python
import functools

import jax
import jax.numpy as jnp
from jax import lax
from jax.experimental import pallas as pl
from jax.experimental.pallas import tpu as pltpu
from jax.sharding import PartitionSpec as P

epsilon = 1e-05
LAG = 3
AHEAD = 4
MESH = pl.DeviceIdType.MESH


def column(row, lanes):
    length = row.shape[1]
    parts = [
        jnp.transpose(jnp.broadcast_to(row[:, a : a + lanes], (lanes, lanes)))
        for a in range(0, length, lanes)
    ]
    return jnp.concatenate(parts, axis=0)


def exact_dot(queries, state):
    high = state.astype(jnp.bfloat16)
    low = (state - high.astype(jnp.float32)).astype(jnp.bfloat16)
    return jnp.dot(
        jnp.concatenate([queries, queries], axis=1),
        jnp.concatenate([high, low], axis=0),
        preferred_element_type=jnp.float32,
    )


def kernel(
    n,
    hn,
    heads,
    hd,
    q_hbm,
    k_hbm,
    v_hbm,
    decay_ref,
    pq_hbm,
    pk_hbm,
    pv_hbm,
    pg_hbm,
    pdecay_ref,
    plen_ref,
    gain_ref,
    dob,
    pob,
    q,
    k,
    v,
    pq,
    pk,
    pv,
    pg,
    dintra,
    pintra,
    cum_t,
    pcum_t,
    closings,
    d0_t,
    d1_t,
    dsuf_t,
    s_out,
    s_own,
    s_in,
    s_first,
    s_chip,
    f_in,
    f_out,
    b_in,
    b_out,
    e_own,
    e_out,
    e_in,
    m_out,
    m_in,
    acc,
    sq,
    scale,
    load_sem,
    close_send,
    close_recv,
    pair_send,
    pair_recv,
    line_send,
    line_recv,
    sq_send,
    sq_recv,
):
    c, r, hx = lax.axis_index("seq"), lax.axis_index("rep"), lax.axis_index("head")
    rows = q.shape[0]
    prow = pq.shape[0]
    count = heads // 2
    blocks = 2 * n
    b = c * 2 + r
    f32 = jnp.float32
    high = lax.Precision.HIGHEST

    loads = [
        pltpu.make_async_copy(src, dst, load_sem.at[i])
        for i, (src, dst) in enumerate(
            [
                (k_hbm, k),
                (v_hbm, v),
                (q_hbm, q),
                (pk_hbm, pk),
                (pq_hbm, pq),
                (pv_hbm, pv),
                (pg_hbm, pg),
            ]
        )
    ]
    for load in loads[:2]:
        load.start()

    barrier = pltpu.get_barrier_semaphore()
    line = []
    for step in range(1, blocks):
        to = lax.rem(b + step, blocks)
        line.append({"seq": to // 2, "rep": lax.rem(to, 2)})
    across = [{"head": lax.rem(hx + step, hn)} for step in range(1, hn)]
    for peer in line + across:
        pl.semaphore_signal(barrier, inc=1, device_id=peer, device_id_type=MESH)

    def upper(length):
        return (
            lax.broadcasted_iota(jnp.int32, (length, length), 0)
            <= lax.broadcasted_iota(jnp.int32, (length, length), 1)
        ).astype(f32)

    contract_rows = (((0,), (0,)), ((), ()))
    contract_lanes = (((1,), (1,)), ((), ()))
    rates = decay_ref[...]
    sums = lax.dot_general(
        jnp.ones((8, rows), f32), rates, contract_lanes, precision=high, preferred_element_type=f32
    )
    closings[b] = jnp.zeros((1, hd), f32)
    closings[b, :, :heads] = sums[0:1]
    cum_t[...] = jnp.dot(rates, upper(rows), precision=high, preferred_element_type=f32)
    pcum_t[...] = jnp.dot(pdecay_ref[...], upper(prow), precision=high, preferred_element_type=f32)
    acc[...] = jnp.zeros_like(acc)

    @pl.when(c == 0)
    def _():
        f_in[...] = jnp.zeros_like(f_in)

    @pl.when(c == n - 1)
    def _():
        b_in[...] = jnp.zeros_like(b_in)

    pl.semaphore_wait(barrier, len(line) + len(across))

    close_copies = [
        pltpu.make_async_remote_copy(
            src_ref=closings.at[b],
            dst_ref=closings.at[b],
            send_sem=close_send.at[i],
            recv_sem=close_recv.at[i],
            device_id=peer,
            device_id_type=MESH,
        )
        for i, peer in enumerate(line)
    ]
    for copy in close_copies:
        copy.start()

    def pair_copy(kind, src, dst, j):
        return pltpu.make_async_remote_copy(
            src_ref=src.at[j],
            dst_ref=dst.at[j],
            send_sem=pair_send.at[kind, j],
            recv_sem=pair_recv.at[kind, j],
            device_id={"rep": 1 - r},
            device_id_type=MESH,
        )

    def line_copy(kind, src, dst, j, to):
        return pltpu.make_async_remote_copy(
            src_ref=src.at[j],
            dst_ref=dst.at[j],
            send_sem=line_send.at[kind, j],
            recv_sem=line_recv.at[kind, j],
            device_id={"seq": to},
            device_id_type=MESH,
        )

    def state_copy(j):
        return pair_copy(0, s_out, s_in, j)

    def entering_copy(j):
        return pair_copy(1, e_out, e_in, j)

    def memory_copy(j):
        return pair_copy(2, m_out, m_in, j)

    right, left = jnp.minimum(c + 1, n - 1), jnp.maximum(c - 1, 0)

    def forward_copy(j):
        return line_copy(0, f_out, f_in, j, right)

    def backward_copy(j):
        return line_copy(1, b_out, b_in, j, left)

    def lanes_of(h):
        return pl.ds(pl.multiple_of(h * hd, hd), hd)

    def own_head(j):
        return r * count + j

    def other_head(j):
        return (1 - r) * count + j

    def state_of(h):
        col = column(cum_t[pl.ds(h, 1), :], hd)
        scaled = (k[:, lanes_of(h)].astype(f32) * jnp.exp(col - col[rows - 1 : rows, :])).astype(
            jnp.bfloat16
        )
        return lax.dot_general(scaled, v[:, lanes_of(h)], contract_rows, preferred_element_type=f32)

    def intra(qs, ks, vs, cums, into, h):
        length = qs.shape[0]
        qh, kh, vh = qs[:, lanes_of(h)], ks[:, lanes_of(h)], vs[:, lanes_of(h)]
        row = cums[pl.ds(h, 1), :]
        col = column(row, hd)
        pieces = []
        for t in range(0, length, hd):
            ends = t + hd
            scores = lax.dot_general(
                qh[t:ends], kh[:ends], contract_lanes, preferred_element_type=f32
            )
            parts = []
            for s in range(0, ends, hd):
                part = scores[:, s : s + hd] * jnp.exp(row[:, s : s + hd] - col[t:ends])
                if s == t:
                    causal = lax.broadcasted_iota(jnp.int32, (hd, hd), 0) >= (
                        lax.broadcasted_iota(jnp.int32, (hd, hd), 1)
                    )
                    part = jnp.where(causal, part, 0.0)
                parts.append(part.astype(jnp.bfloat16))
            weights = jnp.concatenate(parts, axis=1)
            pieces.append(jnp.dot(weights, vh[:ends], preferred_element_type=f32))
        into[h] = jnp.concatenate(pieces, axis=0)

    def finish(h, entering, memory):
        grow = column(jnp.exp(-cum_t[pl.ds(h, 1), :]), hd)
        at = lanes_of(h)
        dob[:, at] = (dintra[h] + grow * exact_dot(q[:, at], entering)).astype(dob.dtype)
        pgrow = column(jnp.exp(-pcum_t[pl.ds(h, 1), :]), hd)
        attended = pintra[h] + pgrow * exact_dot(pq[:, at], memory)
        acc[...] += attended * attended
        pintra[h] = attended * (gain_ref[:, at] * jax.nn.sigmoid(pg[:, at].astype(f32)))

    def combine(j):
        state_copy(j).wait_recv()
        one = jnp.where(r == 0, s_own[j], s_in[j])
        two = jnp.where(r == 0, s_in[j], s_own[j])
        s_first[j] = one
        s_chip[j] = d1_t[pl.ds(own_head(j), 1), :] * one + two

    def forward(j):
        h = own_head(j)

        @pl.when(c > 0)
        def _():
            forward_copy(j).wait_recv()

        before = f_in[j]
        d0, d1 = d0_t[pl.ds(h, 1), :], d1_t[pl.ds(h, 1), :]
        f_out[j] = (d0 * d1) * before + s_chip[j]

        @pl.when(c < n - 1)
        def _():
            forward_copy(j).start()

        second = d0 * before + s_first[j]
        e_own[j] = jnp.where(r == 0, before, second)
        e_out[j] = jnp.where(r == 0, second, before)
        entering_copy(j).start()

    def backward(j):
        @pl.when(c < n - 1)
        def _():
            backward_copy(j).wait_recv()

        @pl.when(c > 0)
        def _():
            b_out[j] = dsuf_t[pl.ds(own_head(j), 1), :] * s_chip[j] + b_in[j]
            backward_copy(j).start()

    @pl.loop(0, count + AHEAD)
    def _(it):
        @pl.when(it == 0)
        def _():
            loads[0].wait()
            loads[1].wait()
            for load in loads[2:]:
                load.start()

        @pl.when(it < count)
        def _():
            s_out[it] = state_of(other_head(it))
            state_copy(it).start()
            s_own[it] = state_of(own_head(it))

        @pl.when(it == AHEAD)
        def _():
            for copy in close_copies:
                copy.wait_recv()
            later = jnp.zeros((1, hd), f32)
            for at in range(2, blocks):
                later = later + jnp.where(at >= 2 * (c + 1), closings[at], 0.0)

            def table(values):
                return jnp.transpose(jnp.broadcast_to(jnp.exp(-values), (hd, hd)))

            d0_t[...] = table(closings[2 * c])
            d1_t[...] = table(closings[2 * c + 1])
            dsuf_t[...] = table(later)

        @pl.when(it >= AHEAD)
        def _():
            j = it - AHEAD
            combine(j)

            @pl.when(c == 0)
            def _():
                forward(j)

            @pl.when(c == n - 1)
            def _():
                backward(j)

    for load in loads[2:]:
        load.wait()

    last = jnp.maximum(jnp.maximum(c - 1, n - 2 - c), 0) * LAG

    @pl.loop(0, count + max(n - 2, 0) * LAG + 1)
    def _(it):
        jf = it - (c - 1) * LAG

        @pl.when((c > 0) & (jf >= 0) & (jf < count))
        def _():
            forward(jf)

        jb = it - (n - 2 - c) * LAG

        @pl.when((c < n - 1) & (jb >= 0) & (jb < count))
        def _():
            backward(jb)

        jm = it - last

        @pl.when((jm >= 0) & (jm < count))
        def _():
            m_out[jm] = dsuf_t[pl.ds(own_head(jm), 1), :] * f_out[jm] + b_in[jm]
            memory_copy(jm).start()

        def begin():
            for h in (own_head(it), other_head(it)):
                intra(q, k, v, cum_t, dintra, h)
                intra(pq, pk, pv, pcum_t, pintra, h)

        jr = jm - 1
        ready = (jr >= 0) & (jr < count)

        def end():
            finish(own_head(jr), e_own[jr], m_out[jr])
            finish(other_head(jr), e_in[jr], m_in[jr])

        @pl.when(ready)
        def _():
            entering_copy(jr).wait_recv()
            memory_copy(jr).wait_recv()

        @pl.when((it < count) & jnp.logical_not(ready))
        def _():
            begin()

        @pl.when((it < count) & ready)
        def _():
            end()
            begin()

        @pl.when((it >= count) & ready)
        def _():
            end()

    squares = lax.dot_general(
        jnp.ones((8, hd), f32), acc[...], contract_lanes, precision=high, preferred_element_type=f32
    )
    sq[hx] = squares
    sq_copies = [
        pltpu.make_async_remote_copy(
            src_ref=sq.at[hx],
            dst_ref=sq.at[hx],
            send_sem=sq_send.at[i],
            recv_sem=sq_recv.at[i],
            device_id=peer,
            device_id_type=MESH,
        )
        for i, peer in enumerate(across)
    ]
    for copy in sq_copies:
        copy.start()
    for copy in sq_copies:
        copy.wait_recv()
    total = sq[0]
    for at in range(1, hn):
        total = total + sq[at]
    factor = lax.rsqrt(total / (hn * heads * hd) + epsilon)
    inside = lax.broadcasted_iota(jnp.int32, factor.shape, 1) < plen_ref[0]
    scale[...] = column(jnp.where(inside, factor, 0.0)[0:1], hd)

    @pl.loop(0, heads)
    def _(h):
        at = lanes_of(h)
        pob[:, at] = (pintra[h] * scale[...]).astype(pob.dtype)

    for copy in close_copies + sq_copies:
        copy.wait_send()

    @pl.loop(0, count)
    def _(j):
        state_copy(j).wait_send()
        entering_copy(j).wait_send()
        memory_copy(j).wait_send()

        @pl.when(c < n - 1)
        def _():
            forward_copy(j).wait_send()

        @pl.when(c > 0)
        def _():
            backward_copy(j).wait_send()


def local(sizes, dq, dk, dv, dd, pq, pk, pv, pg, pd, plen, gain):
    n, hn, reps = sizes
    heads = dd.shape[1]
    rows, width = dq.shape
    hd = width // heads
    passages, prow = pq.shape[:2]
    assert passages == 1 and reps == 2 and heads % 2 == 0 and heads <= hd
    count = heads // 2
    f32, bf16 = jnp.float32, jnp.bfloat16
    pq, pk, pv, pg = (x.reshape(prow, width) for x in (pq, pk, pv, pg))
    anywhere = pl.BlockSpec(memory_space=pl.ANY)
    vmem = pl.BlockSpec(memory_space=pltpu.VMEM)
    smem = pl.BlockSpec(memory_space=pltpu.SMEM)
    blocks = n * reps
    chunks = pltpu.VMEM((count, hd, hd), f32)
    dma = pltpu.SemaphoreType.DMA
    out, pout = pl.pallas_call(
        functools.partial(kernel, n, hn, heads, hd),
        out_shape=(
            pltpu.VMEM((rows, width), bf16),
            pltpu.VMEM((prow, width), bf16),
        ),
        in_specs=[anywhere] * 3 + [vmem] + [anywhere] * 4 + [vmem, smem, vmem],
        out_specs=(vmem, vmem),
        scratch_shapes=[pltpu.VMEM((rows, width), bf16)] * 3
        + [pltpu.VMEM((prow, width), bf16)] * 4
        + [pltpu.VMEM((heads, rows, hd), f32), pltpu.VMEM((heads, prow, hd), f32)]
        + [pltpu.VMEM((heads, rows), f32), pltpu.VMEM((heads, prow), f32)]
        + [pltpu.VMEM((blocks, 1, hd), f32)]
        + [pltpu.VMEM((hd, hd), f32)] * 3
        + [chunks] * 14
        + [pltpu.VMEM((prow, hd), f32), pltpu.VMEM((hn, 8, prow), f32), pltpu.VMEM((prow, hd), f32)]
        + [
            dma((7,)),
            dma((blocks - 1,)),
            dma((blocks - 1,)),
            dma((3, count)),
            dma((3, count)),
            dma((2, count)),
            dma((2, count)),
            dma((max(hn - 1, 1),)),
            dma((max(hn - 1, 1),)),
        ],
        compiler_params=pltpu.CompilerParams(
            collective_id=0, has_side_effects=True, vmem_limit_bytes=50 << 20
        ),
    )(dq, dk, dv, dd.T, pq, pk, pv, pg, pd.reshape(prow, heads).T, plen, gain.reshape(1, width))
    return out, pout.reshape(passages, prow, width)


def solution(mesh):
    rows = ("groups", "seq", "rep")
    flat, deep = P(rows, "head"), P(rows, None, "head")
    sizes = tuple(mesh.shape[axis] for axis in ("seq", "head", "rep"))
    return jax.shard_map(
        functools.partial(local, sizes),
        mesh=mesh,
        in_specs=(flat,) * 4 + (deep,) * 5 + (P(rows), P("head")),
        out_specs=(flat, deep),
        check_vma=False,
    )
```
